256 devices in a mesh: seq: 64 (over x, y_lo, z), ch: 4 (over y_hi, core).
Axes of the slice: x: 4, y: 4 (y_hi: 2, y_lo: 2; y = y_hi * 2 + y_lo), z: 8, core: 2. Of those that a mesh axis runs over, the one named last changes fastest.
Arguments:
- projected: bfloat16 [8192, 3, 4096], P('seq', None, 'ch'), may hold values from -6 to 6
- cotangent: bfloat16 [8192, 4096], P('seq', 'ch'), may hold values from -6 to 6
- short_weight: float32 [3, 7, 4096], P(None, None, 'ch'), may hold values from -2 to 2
- long_filter: float32 [8, 8192], P('ch', 'seq'), may hold values from -0.0625 to 0.0625
Outputs:
- grad_proj: bfloat16 [8192, 3, 4096], P('seq', None, 'ch')
- grad_short: float32 [3, 7, 4096], P(None, None, 'ch')
- grad_filter: float32 [8, 8192], P(None, ('seq', 'ch'))
The draws below stay inside these ranges and needn't reach their ends.
All inputs are finite; a program needn't handle non-finite values.
Results may differ from the reference program's by a relative error of at most 0.00155.
Values may be sent and summed in bfloat16 or wider, within the bound.
No kernel may reach another device: no remote copies, remote signals or barrier semaphores. Data moves between devices by JAX's collectives and lax.ppermute only.
A program may use at most 64 MiB of HBM per device.

```python
import math
import jax
import jax.numpy as jnp
from jax import lax

D = 4096
GROUPS = 8
KSHORT = 7
TOKENS = 8192


def level_of(rng, extent, pieces, smallest, top_value):
    loudness = 1.0
    for dim, shards_of in pieces:
        steps = jax.random.uniform(jax.random.fold_in(jax.random.fold_in(rng, 6), dim), (shards_of,), jnp.float32, smallest / len(pieces), top_value / len(pieces))
        loudness = loudness * jnp.repeat(jnp.exp(steps), extent[dim] // shards_of).reshape((-1,) + (1,) * (len(extent) - 1 - dim))
    return loudness


def centred(key, dims, width, reach, shards=(), held_as=jnp.bfloat16):
    loudness = level_of(key, dims, shards, -0.22, 0.18) if shards else 1.0
    entries = jax.random.normal(key, dims, jnp.float32) * width * loudness
    return jnp.minimum(jnp.maximum(entries, -reach), reach).astype(held_as)


def setup_inputs(seed: int = 0) -> dict:
    arg_keys = jax.random.split(jax.random.key(seed), 5)
    projected = centred(arg_keys[0], (TOKENS, 3, D), 1.0, 6.0, ((0, 64), (2, 4)))
    cotangent = centred(arg_keys[1], (TOKENS, D), 1.0, 6.0, ((0, 64), (1, 4)))
    short_weight = centred(arg_keys[2], (3, KSHORT, D), KSHORT ** -0.5, 2.0, ((2, 4),), jnp.float32)
    long_filter = centred(arg_keys[3], (GROUPS, TOKENS), TOKENS ** -0.5, 0.0625, ((0, 4), (1, 64)), jnp.float32)
    return dict(projected=projected, cotangent=cotangent, short_weight=short_weight, long_filter=long_filter)


def group_backward(proj_group, grad_group, weight_group, filter_group):
    tap_count = weight_group.shape[1]
    channels = proj_group.shape[2]
    padded = jnp.concatenate([jnp.zeros((tap_count - 1, 3, channels), jnp.float32), proj_group], 0)
    features = jnp.zeros((TOKENS, 3, channels), jnp.float32)
    for offset in range(tap_count):
        first_row = tap_count - 1 - offset
        features = features + weight_group[:, offset, :][None] * padded[first_row:first_row + TOKENS]
    mixed_input = features[:, 1] * features[:, 2]
    gated_grad = grad_group * features[:, 0]
    length = 2 * TOKENS
    filter_spec = jnp.fft.rfft(filter_group, n=length)[:, None]
    mixed_spec = jnp.fft.rfft(mixed_input, n=length, axis=0)
    gated_spec = jnp.fft.rfft(gated_grad, n=length, axis=0)
    conv_out = jnp.fft.irfft(filter_spec * mixed_spec, n=length, axis=0)[:TOKENS]
    corr_out = jnp.fft.irfft(jnp.conj(filter_spec) * gated_spec, n=length, axis=0)[:TOKENS]
    cross_spec = lax.optimization_barrier(jnp.sum(jnp.conj(mixed_spec) * gated_spec, axis=1))
    filter_grad = jnp.fft.irfft(cross_spec, n=length)[:TOKENS]
    feat_grad = jnp.stack([grad_group * conv_out, corr_out * features[:, 2], corr_out * features[:, 1]], 1)
    padded_grad = jnp.concatenate([feat_grad, jnp.zeros((tap_count - 1, 3, channels), jnp.float32)], 0)
    grad_proj = jnp.zeros((TOKENS, 3, channels), jnp.float32)
    for offset in range(tap_count):
        grad_proj = grad_proj + weight_group[:, offset, :][None] * padded_grad[offset:offset + TOKENS]
    short_terms = []
    for offset in range(tap_count):
        first_row = tap_count - 1 - offset
        short_terms.append(lax.optimization_barrier(jnp.sum(feat_grad * padded[first_row:first_row + TOKENS], axis=0)))
    grad_short = jnp.stack(short_terms, 1) * (1.0 / math.sqrt(TOKENS))
    filter_grad = filter_grad * (1.0 / math.sqrt(TOKENS * channels))
    return (grad_proj.astype(jnp.bfloat16), grad_short, filter_grad)

def reference(projected, cotangent, short_weight, long_filter):
    group_width = D // GROUPS

    def one_group(group_index):
        first_col = group_index * group_width
        proj_group = lax.dynamic_slice_in_dim(projected, first_col, group_width, 2).astype(jnp.float32)
        grad_group = lax.dynamic_slice_in_dim(cotangent, first_col, group_width, 1).astype(jnp.float32)
        weight_group = lax.dynamic_slice_in_dim(short_weight, first_col, group_width, 2)
        filter_group = lax.dynamic_index_in_dim(long_filter, group_index, 0, keepdims=False)
        return group_backward(proj_group, grad_group, weight_group, filter_group)
    grad_proj, grad_short, grad_filter = lax.map(one_group, jnp.arange(GROUPS, dtype=jnp.int32))
    grad_proj = jnp.transpose(grad_proj, (1, 2, 0, 3)).reshape(TOKENS, 3, D)
    grad_short = jnp.transpose(grad_short, (1, 2, 0, 3)).reshape(3, KSHORT, D)
    return (grad_proj, grad_short, grad_filter)
```

```python
import math

import jax
import jax.numpy as jnp
from jax import lax
from jax.experimental import pallas as pl
from jax.experimental.pallas import tpu as pltpu
from jax.sharding import PartitionSpec as P

f32 = jnp.float32
bf16 = jnp.bfloat16

BLK = 128
NBLK = 64
CH = 16
TAPS = 7
ROWS_IN = 72
ROWS_OUT = 56


def iota(shape, dim):
    return lax.broadcasted_iota(jnp.int32, shape, dim)


def split(x):
    hi = x.astype(bf16)
    return hi, (x - hi.astype(f32)).astype(bf16)


def flip_matrix(n):
    return jnp.where(iota((n, n), 0) + iota((n, n), 1) == n - 1, 1.0, 0.0).astype(bf16)


def dot(a, b):
    return jnp.dot(a, b, preferred_element_type=f32)


def pack_kernel(proj, cot, filt, out):
    for stream in range(4):
        block = proj[stream] if stream < 3 else cot[...]
        turned = block.astype(f32).T.astype(bf16)
        out[:, stream * CH : (stream + 1) * CH, :] = turned.reshape(NBLK, CH, BLK)
    row = iota((8, BLK), 0)
    for group in range(2):
        taps = filt[group : group + 1, :]
        hi = taps.astype(bf16).astype(f32)
        lo = taps - hi
        tile = jnp.where(row == 0, hi, jnp.where(row == 1, lo, 0.0)).astype(bf16)
        half = NBLK // 2
        out[group * half : (group + 1) * half, 4 * CH : ROWS_IN, :] = jnp.broadcast_to(
            tile[None], (half, 8, BLK)
        )


def main_kernel(
    recv, wide, out, toep_hi, toep_lo, zed, mixed, mixt, gsp, gleft, feat1, feat2, acc, crs, corr, diag, rrev, rlow, grads
):
    lane = iota((CH, BLK), 1)
    lane_sq = iota((BLK, BLK), 1)
    row_sq = iota((BLK, BLK), 0)
    keep = lane_sq >= row_sq
    flip2 = flip_matrix(2 * BLK)
    flip1 = flip_matrix(BLK)

    toep_hi[0] = jnp.zeros((BLK, BLK), bf16)
    toep_lo[0] = jnp.zeros((BLK, BLK), bf16)

    def build(m, before):
        pair = recv[m, 4 * CH : ROWS_IN, :].astype(f32)
        taps = pair[0:1] + pair[1:2]
        turned = pltpu.roll(jnp.broadcast_to(taps, (BLK, BLK)), 0, 1, stride=1, stride_axis=0)
        hi, lo = split(jnp.where(keep, turned, before))
        toep_hi[m + 1] = hi
        toep_lo[m + 1] = lo
        return turned

    lax.fori_loop(0, NBLK, build, jnp.zeros((BLK, BLK), f32))

    def featurize(pair_index, before):
        for half in range(2):
            b = pair_index * 2 + half
            current = tuple(recv[b, j * CH : (j + 1) * CH, :].astype(f32) for j in range(3))
            feats = []
            for j in range(3):
                total = wide[j * TAPS] * current[j]
                for k in range(1, TAPS):
                    source = jnp.where(lane < BLK - k, current[j], before[j])
                    total = total + wide[j * TAPS + k] * pltpu.roll(source, k, 1)
                feats.append(total)
            feat1[b] = feats[1]
            feat2[b] = feats[2]
            mix = feats[1] * feats[2]
            gate = recv[b, 3 * CH : 4 * CH, :].astype(f32) * feats[0]
            cols = slice(half * BLK, (half + 1) * BLK)
            cols_lo = slice((2 + half) * BLK, (3 + half) * BLK)
            at = pl.ds(pl.multiple_of(pair_index * CH, CH), CH)
            mixed[at, cols] = mix
            hi, lo = split(mix)
            at_z = pl.ds(pl.multiple_of(pair_index * 2 * CH, CH), CH)
            zed[at_z, cols] = hi
            zed[at_z, cols_lo] = lo
            hi, lo = split(gate)
            gsp[at, cols] = hi
            gsp[at, cols_lo] = lo
            before = current
        return before

    zero = jnp.zeros((CH, BLK), f32)
    lax.fori_loop(0, NBLK // 2, featurize, (zero, zero, zero))

    rows = NBLK // 2 * CH
    width = 2 * BLK
    for part in range(rows // BLK):
        at = slice(part * BLK, (part + 1) * BLK)
        hi, lo = split(mixed[at, :].T)
        mixt[0, :, at] = hi
        mixt[1, :, at] = lo
    for half in range(2):
        cols = slice(half * width, (half + 1) * width)
        gleft[half, 0:rows, :] = dot(gsp[:, cols], flip2).astype(bf16)
        gleft[half, rows : 2 * rows, :] = jnp.zeros((rows, width), bf16)
        for b in range(NBLK // 2):
            back = NBLK // 2 - 1 - b
            zed[2 * CH * back + CH : 2 * CH * back + 2 * CH, cols] = gleft[half, b * CH : (b + 1) * CH, :]

    last = None
    for d in range(NBLK // 2):
        depth = rows if d < NBLK // 4 else rows // 2
        at = slice(CH * d, CH * d + depth)
        left = jnp.concatenate([mixt[0, :, 0:depth], mixt[1, :, 0:depth], mixt[0, :, 0:depth]], 1)
        right = jnp.concatenate([gleft[0, at, :], gleft[0, at, :], gleft[1, at, :]], 0)
        prod = dot(left, right)
        diag[2 * d] = prod[0:BLK, BLK:] + prod[BLK:, 0:BLK]
        if d > 0:
            diag[2 * d - 1] = last + prod[BLK:, BLK:]
        last = prod[0:BLK, 0:BLK]
    diag[NBLK - 1] = last

    def along(step, after):
        q = NBLK - 1 - step
        turned = pltpu.roll(diag[q], 0, 1, stride=1, stride_axis=0)
        picked = jnp.where(keep, turned, after)
        rrev[pl.ds(q, 1), :] = jnp.sum(picked, 0, keepdims=True)
        return turned

    lax.fori_loop(0, NBLK, along, jnp.zeros((BLK, BLK), f32))
    hi, lo = split(rrev[...])
    rrev[0:NBLK, :] = dot(hi, flip1)
    rlow[...] = dot(lo, flip1)

    for d in range(NBLK // 2):
        count = 2 * rows - 2 * CH * d
        hi = jnp.concatenate(
            [
                jnp.concatenate([toep_hi[2 * d + 1], toep_hi[2 * d + 2]], 1),
                jnp.concatenate([toep_hi[2 * d], toep_hi[2 * d + 1]], 1),
            ],
            0,
        )
        lo = jnp.concatenate(
            [
                jnp.concatenate([toep_lo[2 * d + 1], toep_lo[2 * d + 2]], 1),
                jnp.concatenate([toep_lo[2 * d], toep_lo[2 * d + 1]], 1),
            ],
            0,
        )
        left = jnp.concatenate([zed[0:count, :], zed[0:count, 0:width]], 1)
        prod = dot(left, jnp.concatenate([hi, hi, lo], 0))
        if d == 0:
            acc[...] = prod
        else:
            acc[2 * CH * d :, :] = acc[2 * CH * d :, :] + prod
    for b in range(NBLK // 2):
        back = NBLK // 2 - 1 - b
        hi, lo = split(acc[2 * CH * back + CH : 2 * CH * back + 2 * CH, :])
        crs[b * CH : (b + 1) * CH, 0:width] = hi
        crs[b * CH : (b + 1) * CH, width:] = lo
    corr[...] = dot(crs[:, 0:width], flip2) + dot(crs[:, width:], flip2)

    def feat_grad(pair_index, carry):
        for half in range(2):
            b = pair_index * 2 + half
            cols = slice(half * BLK, (half + 1) * BLK)
            conv_part = acc[pl.ds(pl.multiple_of(pair_index * 2 * CH, CH), CH), cols]
            corr_part = corr[pl.ds(pl.multiple_of(pair_index * CH, CH), CH), cols]
            grads[0, b] = recv[b, 3 * CH : 4 * CH, :].astype(f32) * conv_part
            grads[1, b] = corr_part * feat2[b]
            grads[2, b] = corr_part * feat1[b]
        return carry

    lax.fori_loop(0, NBLK // 2, feat_grad, 0)
    short = jnp.zeros((CH, BLK), f32)
    for j in range(3):
        grads[j, NBLK] = zero

        def finish(b, sums, j=j):
            here, there = grads[j, b], grads[j, b + 1]
            given = recv[b, j * CH : (j + 1) * CH, :].astype(f32)
            total = wide[j * TAPS] * here
            fresh = [sums[0] + here * given]
            for k in range(1, TAPS):
                moved = pltpu.roll(jnp.where(lane >= k, here, there), BLK - k, 1)
                total = total + wide[j * TAPS + k] * moved
                fresh.append(sums[k] + moved * given)
            out[b, j * CH : (j + 1) * CH, :] = total.astype(bf16)
            return tuple(fresh)

        sums = lax.fori_loop(0, NBLK, finish, (zero,) * TAPS)
        for k in range(TAPS):
            short = jnp.where(lane == j * TAPS + k, jnp.sum(sums[k], 1, keepdims=True), short)

    row8 = iota((8, BLK), 0)
    tile = jnp.zeros((8, BLK), f32)
    mine = lane % CH == iota((CH, BLK), 0)
    for place, piece in enumerate(split(short)):
        for r in range(3):
            pick = jnp.where(row_sq == 8 * r + lane_sq // CH, 1.0, 0.0).astype(bf16)
            flat = jnp.sum(jnp.where(mine, dot(piece, pick), 0.0), 0, keepdims=True)
            tile = jnp.where(row8 == 2 + 3 * place + r, flat, tile)

    def tail(d, carry):
        high = rrev[pl.ds(d, 1), :]
        low = rlow[pl.ds(d, 1), :]
        whole = jnp.where(row8 == 0, high, jnp.where(row8 == 1, low, tile))
        out[d, 3 * CH : ROWS_OUT, :] = whole.astype(bf16)
        return carry

    lax.fori_loop(0, NBLK, tail, 0)


def unpack_kernel(recv, proj, short, filt):
    for j in range(3):
        block = recv[:, j * CH : (j + 1) * CH, :].reshape(NBLK * CH, BLK)
        proj[j] = block.astype(f32).T.astype(bf16)
    tail = recv[:, 3 * CH : ROWS_OUT, :].astype(f32)
    short[...] = tail[:, 2:5, :] + tail[:, 5:8, :]
    half = NBLK // 2
    for group in range(2):
        part = tail[group * half : (group + 1) * half]
        total = jnp.sum(part, 0)
        filt[group : group + 1, :] = total[0:1] + total[1:2]


def call(kernel, out_shape, scratch=()):
    return pl.pallas_call(kernel, out_shape=out_shape, scratch_shapes=list(scratch))


def pack(proj, cot, filt):
    return call(pack_kernel, jax.ShapeDtypeStruct((NBLK, ROWS_IN, BLK), bf16))(proj, cot, filt)


def middle(recv, wide, interpret=False):
    rows = NBLK // 2 * CH
    width = 2 * BLK
    vmem = pltpu.VMEM
    return pl.pallas_call(
        main_kernel,
        out_shape=jax.ShapeDtypeStruct((NBLK, ROWS_OUT, BLK), bf16),
        scratch_shapes=[
            vmem((NBLK + 1, BLK, BLK), bf16),
            vmem((NBLK + 1, BLK, BLK), bf16),
            vmem((2 * rows, 2 * width), bf16),
            vmem((rows, width), f32),
            vmem((2, width, rows), bf16),
            vmem((rows, 2 * width), bf16),
            vmem((2, 2 * rows, width), bf16),
            vmem((NBLK, CH, BLK), f32),
            vmem((NBLK, CH, BLK), f32),
            vmem((2 * rows, width), f32),
            vmem((rows, 2 * width), bf16),
            vmem((rows, width), f32),
            vmem((NBLK, BLK, BLK), f32),
            vmem((NBLK, BLK), f32),
            vmem((NBLK, BLK), f32),
            vmem((3, NBLK + 1, CH, BLK), f32),
        ],
        interpret=interpret,
    )(recv, wide)


def local(projected, cotangent, short_weight, long_filter):
    chan_count = projected.shape[2]
    token_count = BLK * NBLK
    sent = pack(jnp.transpose(projected, (1, 0, 2)), cotangent, long_filter)
    recv = lax.all_to_all(sent, "seq", split_axis=0, concat_axis=0, tiled=True)
    mine = lax.dynamic_slice_in_dim(
        short_weight.reshape(3 * TAPS, chan_count), lax.axis_index("seq") * CH, CH, 1
    )
    wide = jnp.broadcast_to(mine[:, :, None], (3 * TAPS, CH, BLK))
    back = middle(recv, wide)
    back = lax.all_to_all(back, "seq", split_axis=0, concat_axis=0, tiled=True)
    proj, short, filt = call(
        unpack_kernel,
        (
            jax.ShapeDtypeStruct((3, BLK, chan_count), bf16),
            jax.ShapeDtypeStruct((NBLK, 3, BLK), f32),
            jax.ShapeDtypeStruct((2, BLK), f32),
        ),
    )(back)
    grad_proj = jnp.transpose(proj, (1, 0, 2))
    short = jnp.transpose(short.reshape(NBLK, 24, CH), (1, 0, 2)).reshape(24, chan_count)
    grad_short = short[: 3 * TAPS].reshape(3, TAPS, chan_count) * (1.0 / math.sqrt(token_count))
    filt = filt * (1.0 / math.sqrt(token_count * (chan_count // 2)))
    grad_filter = lax.all_to_all(filt, "ch", split_axis=1, concat_axis=0, tiled=True)
    return (grad_proj, grad_short, grad_filter)


def solution(mesh):
    return jax.shard_map(
        local,
        mesh=mesh,
        in_specs=(P("seq", None, "ch"), P("seq", "ch"), P(None, None, "ch"), P("ch", "seq")),
        out_specs=(P("seq", None, "ch"), P(None, None, "ch"), P(None, ("seq", "ch"))),
        check_vma=False,
    )
```

```python
import math

import jax
import jax.numpy as jnp
from jax import lax
from jax.experimental import pallas as pl
from jax.experimental.pallas import tpu as pltpu
from jax.sharding import PartitionSpec as P

f32 = jnp.float32
bf16 = jnp.bfloat16

BLK = 128
NBLK = 64
CH = 16
TAPS = 7
ROWS_IN = 72
ROWS_OUT = 56


def iota(shape, dim):
    return lax.broadcasted_iota(jnp.int32, shape, dim)


def split(x):
    hi = x.astype(bf16)
    return hi, (x - hi.astype(f32)).astype(bf16)


def flip_matrix(n):
    return jnp.where(iota((n, n), 0) + iota((n, n), 1) == n - 1, 1.0, 0.0).astype(bf16)


def dot(a, b):
    return jnp.dot(a, b, preferred_element_type=f32)


def pack_kernel(proj, cot, filt, out):
    for stream in range(4):
        block = proj[stream] if stream < 3 else cot[...]
        turned = block.astype(f32).T.astype(bf16)
        out[:, stream * CH : (stream + 1) * CH, :] = turned.reshape(NBLK, CH, BLK)
    row = iota((8, BLK), 0)
    for group in range(2):
        taps = filt[group : group + 1, :]
        hi = taps.astype(bf16).astype(f32)
        lo = taps - hi
        tile = jnp.where(row == 0, hi, jnp.where(row == 1, lo, 0.0)).astype(bf16)
        half = NBLK // 2
        out[group * half : (group + 1) * half, 4 * CH : ROWS_IN, :] = jnp.broadcast_to(
            tile[None], (half, 8, BLK)
        )


def main_kernel(
    recv, wide, out, toep_hi, toep_lo, zed, mixed, mixt, gsp, gleft, feat1, feat2, acc, crs, corr, diag, rrev, rlow, grads
):
    lane = iota((CH, BLK), 1)
    lane_sq = iota((BLK, BLK), 1)
    row_sq = iota((BLK, BLK), 0)
    keep = lane_sq >= row_sq
    flip2 = flip_matrix(2 * BLK)
    flip1 = flip_matrix(BLK)

    toep_hi[0] = jnp.zeros((BLK, BLK), bf16)
    toep_lo[0] = jnp.zeros((BLK, BLK), bf16)

    def build(m, before):
        pair = recv[m, 4 * CH : ROWS_IN, :].astype(f32)
        taps = pair[0:1] + pair[1:2]
        turned = pltpu.roll(jnp.broadcast_to(taps, (BLK, BLK)), 0, 1, stride=1, stride_axis=0)
        hi, lo = split(jnp.where(keep, turned, before))
        toep_hi[m + 1] = hi
        toep_lo[m + 1] = lo
        return turned

    lax.fori_loop(0, NBLK, build, jnp.zeros((BLK, BLK), f32), unroll=8)

    def featurize(pair_index, before):
        for half in range(2):
            b = pair_index * 2 + half
            current = tuple(recv[b, j * CH : (j + 1) * CH, :].astype(f32) for j in range(3))
            feats = []
            for j in range(3):
                total = wide[j * TAPS] * current[j]
                for k in range(1, TAPS):
                    source = jnp.where(lane < BLK - k, current[j], before[j])
                    total = total + wide[j * TAPS + k] * pltpu.roll(source, k, 1)
                feats.append(total)
            feat1[b] = feats[1]
            feat2[b] = feats[2]
            mix = feats[1] * feats[2]
            gate = recv[b, 3 * CH : 4 * CH, :].astype(f32) * feats[0]
            cols = slice(half * BLK, (half + 1) * BLK)
            cols_lo = slice((2 + half) * BLK, (3 + half) * BLK)
            at = pl.ds(pl.multiple_of(pair_index * CH, CH), CH)
            mixed[at, cols] = mix
            hi, lo = split(mix)
            at_z = pl.ds(pl.multiple_of(pair_index * 2 * CH, CH), CH)
            zed[at_z, cols] = hi
            zed[at_z, cols_lo] = lo
            hi, lo = split(gate)
            gsp[at, cols] = hi
            gsp[at, cols_lo] = lo
            before = current
        return before

    zero = jnp.zeros((CH, BLK), f32)
    lax.fori_loop(0, NBLK // 2, featurize, (zero, zero, zero), unroll=4)

    rows = NBLK // 2 * CH
    width = 2 * BLK
    for part in range(rows // BLK):
        at = slice(part * BLK, (part + 1) * BLK)
        hi, lo = split(mixed[at, :].T)
        mixt[0, :, at] = hi
        mixt[1, :, at] = lo
    for half in range(2):
        cols = slice(half * width, (half + 1) * width)
        gleft[half, 0:rows, :] = dot(gsp[:, cols], flip2).astype(bf16)
        gleft[half, rows : 2 * rows, :] = jnp.zeros((rows, width), bf16)
        for b in range(NBLK // 2):
            back = NBLK // 2 - 1 - b
            zed[2 * CH * back + CH : 2 * CH * back + 2 * CH, cols] = gleft[half, b * CH : (b + 1) * CH, :]

    last = None
    for d in range(NBLK // 2):
        depth = rows if d < NBLK // 4 else rows // 2
        at = slice(CH * d, CH * d + depth)
        left = jnp.concatenate([mixt[0, :, 0:depth], mixt[1, :, 0:depth], mixt[0, :, 0:depth]], 1)
        right = jnp.concatenate([gleft[0, at, :], gleft[0, at, :], gleft[1, at, :]], 0)
        prod = dot(left, right)
        diag[2 * d] = prod[0:BLK, BLK:] + prod[BLK:, 0:BLK]
        if d > 0:
            diag[2 * d - 1] = last + prod[BLK:, BLK:]
        last = prod[0:BLK, 0:BLK]
    diag[NBLK - 1] = last

    def along(step, after):
        q = NBLK - 1 - step
        turned = pltpu.roll(diag[q], 0, 1, stride=1, stride_axis=0)
        picked = jnp.where(keep, turned, after)
        rrev[pl.ds(q, 1), :] = jnp.sum(picked, 0, keepdims=True)
        return turned

    lax.fori_loop(0, NBLK, along, jnp.zeros((BLK, BLK), f32), unroll=8)
    hi, lo = split(rrev[...])
    rrev[0:NBLK, :] = dot(hi, flip1)
    rlow[...] = dot(lo, flip1)

    for d in range(NBLK // 2):
        count = 2 * rows - 2 * CH * d
        hi = jnp.concatenate(
            [
                jnp.concatenate([toep_hi[2 * d + 1], toep_hi[2 * d + 2]], 1),
                jnp.concatenate([toep_hi[2 * d], toep_hi[2 * d + 1]], 1),
            ],
            0,
        )
        lo = jnp.concatenate(
            [
                jnp.concatenate([toep_lo[2 * d + 1], toep_lo[2 * d + 2]], 1),
                jnp.concatenate([toep_lo[2 * d], toep_lo[2 * d + 1]], 1),
            ],
            0,
        )
        left = jnp.concatenate([zed[0:count, :], zed[0:count, 0:width]], 1)
        prod = dot(left, jnp.concatenate([hi, hi, lo], 0))
        if d == 0:
            acc[...] = prod
        else:
            acc[2 * CH * d :, :] = acc[2 * CH * d :, :] + prod
    for b in range(NBLK // 2):
        back = NBLK // 2 - 1 - b
        hi, lo = split(acc[2 * CH * back + CH : 2 * CH * back + 2 * CH, :])
        crs[b * CH : (b + 1) * CH, 0:width] = hi
        crs[b * CH : (b + 1) * CH, width:] = lo
    corr[...] = dot(crs[:, 0:width], flip2) + dot(crs[:, width:], flip2)

    def feat_grad(pair_index, carry):
        for half in range(2):
            b = pair_index * 2 + half
            cols = slice(half * BLK, (half + 1) * BLK)
            conv_part = acc[pl.ds(pl.multiple_of(pair_index * 2 * CH, CH), CH), cols]
            corr_part = corr[pl.ds(pl.multiple_of(pair_index * CH, CH), CH), cols]
            grads[0, b] = recv[b, 3 * CH : 4 * CH, :].astype(f32) * conv_part
            grads[1, b] = corr_part * feat2[b]
            grads[2, b] = corr_part * feat1[b]
        return carry

    lax.fori_loop(0, NBLK // 2, feat_grad, 0, unroll=4)
    short = jnp.zeros((CH, BLK), f32)
    for j in range(3):
        grads[j, NBLK] = zero

        def finish(b, sums, j=j):
            here, there = grads[j, b], grads[j, b + 1]
            given = recv[b, j * CH : (j + 1) * CH, :].astype(f32)
            total = wide[j * TAPS] * here
            fresh = [sums[0] + here * given]
            for k in range(1, TAPS):
                moved = pltpu.roll(jnp.where(lane >= k, here, there), BLK - k, 1)
                total = total + wide[j * TAPS + k] * moved
                fresh.append(sums[k] + moved * given)
            out[b, j * CH : (j + 1) * CH, :] = total.astype(bf16)
            return tuple(fresh)

        sums = lax.fori_loop(0, NBLK, finish, (zero,) * TAPS, unroll=16)
        for k in range(TAPS):
            short = jnp.where(lane == j * TAPS + k, jnp.sum(sums[k], 1, keepdims=True), short)

    row8 = iota((8, BLK), 0)
    tile = jnp.zeros((8, BLK), f32)
    mine = lane % CH == iota((CH, BLK), 0)
    for place, piece in enumerate(split(short)):
        for r in range(3):
            pick = jnp.where(row_sq == 8 * r + lane_sq // CH, 1.0, 0.0).astype(bf16)
            flat = jnp.sum(jnp.where(mine, dot(piece, pick), 0.0), 0, keepdims=True)
            tile = jnp.where(row8 == 2 + 3 * place + r, flat, tile)

    def tail(d, carry):
        high = rrev[pl.ds(d, 1), :]
        low = rlow[pl.ds(d, 1), :]
        whole = jnp.where(row8 == 0, high, jnp.where(row8 == 1, low, tile))
        out[d, 3 * CH : ROWS_OUT, :] = whole.astype(bf16)
        return carry

    lax.fori_loop(0, NBLK, tail, 0, unroll=8)


def reduce_kernel(tail, filt):
    half = NBLK // 2
    scale = 1.0 / math.sqrt(BLK * NBLK * CH * half)
    row = iota((8, BLK), 0)
    totals = []
    for group in range(2):
        total = jnp.sum(tail[group * half : (group + 1) * half].astype(f32), 0)
        totals.append((total[0:1] + total[1:2]) * scale)
    both = jnp.where(row == 0, totals[0], totals[1])
    for piece in range(4):
        filt[piece] = both if piece == 0 else pltpu.roll(both, BLK - piece * (BLK // 4), 1)


def unpack_kernel(recv, proj, short):
    chans = NBLK * CH
    for j in range(3):
        block = recv[:, j * CH : (j + 1) * CH, :].reshape(chans, BLK)
        proj[j] = block.astype(f32).T.astype(bf16)
    tail = recv[:, 3 * CH : ROWS_OUT, :].astype(f32)
    spread = jnp.where(iota((NBLK, chans), 1) // CH == iota((NBLK, chans), 0), 1.0, 0.0).astype(bf16)
    own = iota((BLK, chans), 0) % CH == iota((BLK, chans), 1) % CH
    gather = jnp.where(iota((8, BLK), 1) // CH == iota((8, BLK), 0), 1.0, 0.0).astype(bf16)
    parts = []
    for r in range(3):
        total = jnp.zeros((8, chans), f32)
        for place in range(2):
            piece = tail[:, 2 + 3 * place + r, :].T.astype(bf16)
            total = total + dot(gather, jnp.where(own, dot(piece, spread), 0.0).astype(bf16))
        parts.append(total)
    whole = jnp.concatenate(parts, 0) * (1.0 / math.sqrt(BLK * NBLK))
    for j in range(3):
        short[j] = whole[j * TAPS : (j + 1) * TAPS]


def call(kernel, out_shape, **rest):
    return pl.pallas_call(kernel, out_shape=out_shape, **rest)


def pack(proj, cot, filt):
    return call(pack_kernel, jax.ShapeDtypeStruct((NBLK, ROWS_IN, BLK), bf16))(proj, cot, filt)


def middle(recv, wide, interpret=False):
    rows = NBLK // 2 * CH
    width = 2 * BLK
    vmem = pltpu.VMEM
    return pl.pallas_call(
        main_kernel,
        out_shape=jax.ShapeDtypeStruct((NBLK, ROWS_OUT, BLK), bf16),
        scratch_shapes=[
            vmem((NBLK + 1, BLK, BLK), bf16),
            vmem((NBLK + 1, BLK, BLK), bf16),
            vmem((2 * rows, 2 * width), bf16),
            vmem((rows, width), f32),
            vmem((2, width, rows), bf16),
            vmem((rows, 2 * width), bf16),
            vmem((2, 2 * rows, width), bf16),
            vmem((NBLK, CH, BLK), f32),
            vmem((NBLK, CH, BLK), f32),
            vmem((2 * rows, width), f32),
            vmem((rows, 2 * width), bf16),
            vmem((rows, width), f32),
            vmem((NBLK, BLK, BLK), f32),
            vmem((NBLK, BLK), f32),
            vmem((NBLK, BLK), f32),
            vmem((3, NBLK + 1, CH, BLK), f32),
        ],
        interpret=interpret,
    )(recv, wide)


def local(projected, cotangent, short_weight, long_filter):
    chan_count = projected.shape[2]
    sent = pack(jnp.transpose(projected, (1, 0, 2)), cotangent, long_filter)
    recv = lax.all_to_all(sent, "seq", split_axis=0, concat_axis=0, tiled=True)
    mine = lax.dynamic_slice_in_dim(
        short_weight.reshape(3 * TAPS, chan_count), lax.axis_index("seq") * CH, CH, 1
    )
    wide = jnp.broadcast_to(mine[:, :, None], (3 * TAPS, CH, BLK))
    back = middle(recv, wide)
    back = lax.all_to_all(back, "seq", split_axis=0, concat_axis=0, tiled=True)
    shares = call(
        reduce_kernel,
        jax.ShapeDtypeStruct((4, 8, BLK), f32),
        grid=(1,),
        in_specs=[pl.BlockSpec((NBLK, 8, BLK), lambda i: (0, 3 * CH // 8, 0))],
        out_specs=pl.BlockSpec((4, 8, BLK), lambda i: (0, 0, 0)),
    )(back)
    owned = lax.all_to_all(shares, "ch", split_axis=0, concat_axis=0, tiled=True)
    proj, grad_short = call(
        unpack_kernel,
        (
            jax.ShapeDtypeStruct((3, BLK, chan_count), bf16),
            jax.ShapeDtypeStruct((3, TAPS, chan_count), f32),
        ),
    )(back)
    grad_proj = jnp.transpose(proj, (1, 0, 2))
    grad_filter = owned[:, 0:2, 0 : BLK // 4].reshape(8, BLK // 4)
    return (grad_proj, grad_short, grad_filter)


def solution(mesh):
    return jax.shard_map(
        local,
        mesh=mesh,
        in_specs=(P("seq", None, "ch"), P("seq", "ch"), P(None, None, "ch"), P("ch", "seq")),
        out_specs=(P("seq", None, "ch"), P(None, None, "ch"), P(None, ("seq", "ch"))),
        check_vma=False,
    )
```
